512 devices in a mesh: dp: 32 (over y, z_lo), expert: 16 (over z_hi, x, core).
Axes of the slice: x: 4, y: 4, z: 16 (z_hi: 2, z_lo: 8; z = z_hi * 8 + z_lo), core: 2. Of those that a mesh axis runs over, the one named last changes fastest.
Arguments:
- tokens: bfloat16 [65536, 2048], P(('dp', 'expert')), may hold values from -6 to 6
- choice_rows: int32 [32, 16, 512], P('dp', 'expert'), may hold values from 0 to 2047, as said below
- gate_weights: float32 [32, 16, 512], P('dp', 'expert'), may hold values from 0.1 to 1
- w_gate: bfloat16 [16, 2048, 1024], P('expert', 'dp'), may hold values from -0.125 to 0.125
- w_up: bfloat16 [16, 2048, 1024], P('expert', 'dp'), may hold values from -0.125 to 0.125
- w_down: bfloat16 [16, 1024, 2048], P('expert', 'dp'), may hold values from -0.1875 to 0.1875
Outputs:
- mixed: bfloat16 [65536, 2048], P(('dp', 'expert'))
The draws below stay inside these ranges and needn't reach their ends.
Inputs may be any that keep to these rules, and one draw needn't show every extreme that they name: `choice_rows`: for each group and expert the 512 numbers are distinct; at most 64 of them lie among the 128 tokens of one device of the group (numbers k * 128 to (k + 1) * 128 - 1 belong to device k of the expert axis), and for every expert and group some device gives exactly 64.
All inputs are finite; a program needn't handle non-finite values.
Results may differ from the reference program's by a relative error of at most 0.0057.
Values may be sent and summed in bfloat16 or wider, within the bound.
A program may use at most 64 MiB of HBM per device.

```python
import jax
import jax.numpy as jnp
from jax import lax

D = 2048
H = 1024
TOK_DEV = 128
EXPERTS = 16
GROUPS = 32
GROUP = 2048
CAP = 512
TOKENS = 65536


def one_expert_rows(key):
    average = TOK_DEV // 4
    parts = jax.random.split(key, 5)
    amounts = jax.random.randint(parts[0], (EXPERTS,), 0, average + 1)
    anchor = jax.random.randint(parts[1], (), 0, EXPERTS)
    offset = jax.random.randint(parts[2], (), 1, EXPERTS)
    amounts = amounts.at[anchor].set(average)
    amounts = amounts.at[(anchor + offset) % EXPERTS].set(0)
    counts = average + amounts - jnp.roll(amounts, -offset)
    orders = jax.vmap(lambda inner: jax.random.permutation(inner, TOK_DEV))(jax.random.split(parts[3], EXPERTS))
    usable = jnp.arange(TOK_DEV)[None, :] < counts[:, None]
    numbers = jnp.arange(EXPERTS)[:, None] * TOK_DEV + orders
    shuffle = jax.random.permutation(parts[4], EXPERTS * TOK_DEV).reshape(EXPERTS, TOK_DEV)
    scores = jnp.where(usable, shuffle, shuffle + EXPERTS * TOK_DEV)
    ranking = jnp.argsort(scores.reshape(-1), stable=True)
    return numbers.reshape(-1)[ranking[:CAP]].astype(jnp.int32)


def draw_choice_rows(key, part):
    keys = jax.random.split(key, GROUPS * EXPERTS)
    picks = jax.vmap(one_expert_rows)(keys)
    return picks.reshape(GROUPS, EXPERTS, CAP)


def steps_of(own_key, dims, cuts, smallest, largest):
    gain, own = 1.0, jax.random.fold_in(own_key, 6)
    for position, blocks in cuts:
        steps = jnp.exp(jax.random.uniform(jax.random.fold_in(own, position), (blocks,), jnp.float32, smallest / len(cuts), largest / len(cuts)))
        gain = gain * jnp.repeat(steps, dims[position] // blocks).reshape([-1 if axis == position else 1 for axis in range(len(dims))])
    return gain


def normal_values(own_key, extent, width, most, pieces=(), dtype=jnp.bfloat16):
    values = jax.random.normal(own_key, extent, jnp.float32) * width
    if len(pieces) > 0:
        values = steps_of(own_key, extent, pieces, -0.22, 0.18) * values
    return jnp.clip(values, min=-most, max=most).astype(dtype)


def setup_inputs(seed: int = 0) -> dict:
    seeds = jax.random.split(jax.random.key(seed), 7)
    return {
        "tokens": normal_values(seeds[0], (TOKENS, D), 1.0, 6.0, ((0, 512),)),
        "choice_rows": draw_choice_rows(jax.random.fold_in(seeds[6], 71), 0),
        "gate_weights": jnp.clip(0.1 + 0.9 * jax.random.uniform(seeds[2], (GROUPS, EXPERTS, CAP), jnp.float32) ** steps_of(seeds[2], (GROUPS, EXPERTS, CAP), ((0, 32), (1, 16)), -0.2, 0.2), 0.1, 1.0),
        "w_gate": normal_values(seeds[3], (EXPERTS, D, H), D ** -0.5, 0.125, ((0, 16), (1, 32))),
        "w_up": normal_values(seeds[4], (EXPERTS, D, H), D ** -0.5, 0.125, ((0, 16), (1, 32))),
        "w_down": normal_values(seeds[5], (EXPERTS, H, D), H ** -0.5, 0.1875, ((0, 16), (1, 32))),
    }


def reference(tokens, choice_rows, gate_weights, w_gate, w_up, w_down):
    grouped = tokens.reshape(GROUPS, GROUP, D)
    gate_full = w_gate.astype(jnp.float32)
    up_full = w_up.astype(jnp.float32)
    down_full = w_down.astype(jnp.float32)

    def one_group(packed):
        group_rows, picks, weights = packed
        picked = group_rows[picks.astype(jnp.int32)].astype(jnp.float32)
        gate = jnp.einsum("ecd,edh->ech", picked, gate_full)
        up_val = jnp.einsum("ecd,edh->ech", picked, up_full)
        hidden = (jax.nn.silu(gate) * up_val).astype(jnp.bfloat16)
        expert_out = jnp.einsum("ech,ehd->ecd", hidden.astype(jnp.float32), down_full)
        contribution = (weights[:, :, None] * expert_out).astype(jnp.bfloat16)
        total = jnp.zeros((GROUP, D), jnp.float32)
        total = total.at[picks.reshape(-1).astype(jnp.int32)].add(contribution.reshape(-1, D).astype(jnp.float32))
        return total.astype(jnp.bfloat16)

    mixed = lax.map(one_group, (grouped, choice_rows, gate_weights))
    return mixed.reshape(TOKENS, D)
```

```python
import functools

import jax
import jax.numpy as jnp
from jax import lax
from jax.experimental import pallas as pl
from jax.experimental.pallas import tpu as pltpu
from jax.sharding import PartitionSpec as P

MESH = pl.DeviceIdType.MESH
Y = 4
X = 4
NC = 4
BF = jnp.bfloat16
F32 = jnp.float32


def remote(src, dst, send_sem, recv_sem, device):
    return pltpu.make_async_remote_copy(
        src_ref=src,
        dst_ref=dst,
        send_sem=send_sem,
        recv_sem=recv_sem,
        device_id=device,
        device_id_type=MESH,
    )


def layer_kernel(
    ZL,
    tin, gu_in, dn_in, rows_col, rows_row, gw_col,
    out,
    tok, gu, dn, oh, oht, picked, hidden, contrib, dense,
    rz, prcv, xrl, xf, zsend, zrel, zfin,
    gsem, dsem, tsem, xsem, psem, csem,
):
    T, D = tin.shape
    H = gu.shape[1] // 2
    CAP = rows_col.shape[0]
    CW = D // NC
    T2 = T // 2
    dp = lax.axis_index("dp")
    ex = lax.axis_index("expert")
    y, k = dp // ZL, dp % ZL
    zh, x, c = ex // (2 * X), (ex // 2) % X, ex % 2
    z = zh * ZL + k
    oz = 1 - zh
    yp, ym, y2 = (y + 1) % Y, (y + 3) % Y, (y + 2) % Y
    xp, xm, x2 = (x + 1) % X, (x + 3) % X, (x + 2) % X
    zq = ((z + ZL // 2) % (2 * ZL), (z + 2 * ZL - ZL // 2) % (2 * ZL))

    def dev(y_=y, k_=k, zh_=zh, x_=x, c_=c):
        return (y_ * ZL + k_, zh_ * (2 * X) + x_ * 2 + c_)

    dev_y = (dev(y_=yp), dev(y_=ym))
    dev_x = (dev(x_=xp), dev(x_=xm))
    dev_z = (dev(k_=k + 1), dev(k_=k - 1))
    dev_q = tuple(dev(k_=v % ZL, zh_=v // ZL) for v in zq)
    dev_c = dev(c_=1 - c)
    has_z = (k < ZL - 1, k > 0)

    barrier = pltpu.get_barrier_semaphore()
    for peer in dev_y + dev_x + dev_q + (dev_c,):
        pl.semaphore_signal(barrier, inc=1, device_id=peer, device_id_type=MESH)
    for d in range(2):
        @pl.when(has_z[d])
        def _():
            pl.semaphore_signal(barrier, inc=1, device_id=dev_z[d], device_id_type=MESH)
    pl.semaphore_wait(barrier, 7 + jnp.where(k < ZL - 1, 1, 0) + jnp.where(k > 0, 1, 0))

    class Part:
        def __init__(self, own, buf, sem):
            self.own, self.buf, self.sem = own, buf, sem
            self.R = own.shape[0]

        def rows(self, y_, j, half=None):
            R = self.R
            if half is None:
                return self.buf.at[pl.ds(pl.multiple_of((y_ * ZL + j) * R, R), R)]
            h = R // 2
            return self.buf.at[pl.ds(pl.multiple_of((y_ * ZL + j) * R + half * h, h), h)]

        def z_send(self, src, j, d):
            remote(src, self.rows(y, j), self.sem.at[1 + d, j], self.sem.at[0, j], dev_z[d]).start()

        def y_send(self, src, j):
            for d in range(2):
                remote(src, self.rows(y, j), self.sem.at[3 + d, j], self.sem.at[5 + d, j], dev_y[d]).start()

        def wait(self, ref, i, j):
            remote(ref, ref, self.sem.at[1, j], self.sem.at[i, j], dev_c).wait_recv()

        def wait_sent(self, ref, i, j):
            remote(ref, ref, self.sem.at[i, j], self.sem.at[0, j], dev_c).wait_send()

        def z_step(self, s, with_y):
            for d, j in ((0, k - s), (1, k + s)):
                @pl.when((j >= 0) & (j < ZL))
                def _():
                    ref = self.rows(y, j)
                    self.wait(ref, 0, j)
                    @pl.when(has_z[d])
                    def _():
                        self.z_send(ref, j, d)
                    if with_y:
                        self.y_send(ref, j)

        def y_step(self, s):
            for d, j in ((0, k - s), (1, k + s)):
                ok = (j >= 0) & (j < ZL)
                if d == 1:
                    ok = ok & (s > 0)
                @pl.when(ok)
                def _():
                    @pl.when(s > 0)
                    def _():
                        self.y_send(self.rows(y, j), j)
                    @pl.when(s == 0)
                    def _():
                        self.y_send(self.own, j)

        def relay_step(self, s):
            for d, j in ((0, k - s), (1, k + s)):
                ok = (j >= 0) & (j < ZL)
                if d == 1:
                    ok = ok & (s > 0)
                @pl.when(ok)
                def _():
                    for e, y_ in ((0, ym), (1, yp)):
                        self.wait(self.rows(y_, j), 5 + e, j)
                        half = self.rows(y_, j, e)
                        remote(half, half, self.sem.at[7 + e, j], self.sem.at[9 + e, j], dev_y[e]).start()

        def arrived(self):
            @pl.loop(0, ZL)
            def _(j):
                for e in range(2):
                    self.wait(self.rows(y2, j, e), 9 + e, j)

        def drain(self):
            @pl.loop(0, ZL)
            def _(j):
                ref = self.rows(y, j)
                for d in range(2):
                    self.wait_sent(ref, 3 + d, j)
                    self.wait_sent(self.rows(y, j, 0), 7 + d, j)
                    ok = has_z[d] & ((j <= k) if d == 0 else (j >= k))
                    @pl.when(ok)
                    def _():
                        self.wait_sent(ref, 1 + d, j)

    G = Part(gu_in, gu, gsem)
    W = Part(dn_in, dn, dsem)

    def blk(c_, x_, q_):
        b = c_ * (2 * X) + x_ * 2 + q_
        return tok.at[pl.ds(pl.multiple_of(b * T, T), T)]

    def blk_half(c_, x_, q_, h):
        b = c_ * (2 * X) + x_ * 2 + q_
        return tok.at[pl.ds(pl.multiple_of(b * T + h * T2, T2), T2)]

    def wait_on(ref, sem):
        remote(ref, ref, sem, sem, dev_c).wait_recv()

    def wait_sent_on(ref, sem):
        remote(ref, ref, sem, sem, dev_c).wait_send()

    def x_send(src, q):
        for d in range(2):
            remote(src, blk(c, x, q), xsem.at[d, q], xsem.at[2 + d, q], dev_x[d]).start()

    def to_partner(src, r, q):
        x_ = (x + r) % X
        remote(src, blk(c, x_, q), psem.at[0, r * 2 + q], psem.at[1, r * 2 + q], dev_c).start()

    def x_arrivals(q):
        for d, r in ((0, 3), (1, 1)):
            ref = blk(c, (x + r) % X, q)
            wait_on(ref, xsem.at[2 + d, q])
            @pl.when(q == d)
            def _():
                remote(ref, ref, xsem.at[4, q], xsem.at[5, q], dev_x[d]).start()
            to_partner(ref, r, q)

    def x_far(q):
        ref = blk(c, x2, q)
        wait_on(ref, xsem.at[5, q])
        to_partner(ref, 2, q)

    def tok_leg1():
        for d in range(2):
            remote(tin.at[pl.ds(d * T2, T2)], rz.at[d], tsem.at[0, d], tsem.at[1, d], dev_q[d]).start()

    def tok_leg2():
        for d in range(2):
            wait_on(rz.at[d], tsem.at[1, d])
            far = 1 - zq[d] // ZL
            remote(rz.at[d], blk_half(c, x, far, d), tsem.at[2, d], tsem.at[3, d], dev_q[d]).start()

    def tok_opp():
        for d in range(2):
            wait_on(blk_half(c, x, oz, d), tsem.at[3, d])
        x_send(blk(c, x, oz), oz)
        to_partner(blk(c, x, oz), 0, oz)

    for d in range(2):
        @pl.when(has_z[d])
        def _():
            G.z_send(gu_in, k, d)
    G.y_send(gu_in, k)
    tok_leg1()
    x_send(tin, zh)
    to_partner(tin, 0, zh)
    for d in range(2):
        @pl.when(has_z[d])
        def _():
            W.z_send(dn_in, k, d)

    gu[pl.ds(pl.multiple_of(dp * gu_in.shape[0], gu_in.shape[0]), gu_in.shape[0]), :] = gu_in[...]
    dn[pl.ds(pl.multiple_of(dp * dn_in.shape[0], dn_in.shape[0]), dn_in.shape[0]), :] = dn_in[...]
    tok[pl.ds(pl.multiple_of((c * 2 * X + x * 2 + zh) * T, T), T), :] = tin[...]

    G.z_step(1, True)

    NB = 2 * X * 2

    @pl.loop(0, NB)
    def _(b):
        off = pl.multiple_of(b * T, T)
        lanes = lax.broadcasted_iota(jnp.int32, (CAP, T), 1) + b * T
        oh[:, pl.ds(off, T)] = jnp.where(rows_col[...] == lanes, 1.0, 0.0).astype(BF)
        subs = lax.broadcasted_iota(jnp.int32, (T, CAP), 0) + b * T
        oht[pl.ds(off, T), :] = jnp.where(rows_row[...] == subs, 1.0, 0.0).astype(BF)

    G.z_step(2, True)
    W.z_step(1, False)
    x_arrivals(zh)
    tok_leg2()
    G.z_step(3, True)
    W.z_step(2, False)
    G.relay_step(0)
    W.y_step(0)
    x_far(zh)
    G.z_step(4, True)
    W.z_step(3, False)
    G.relay_step(1)
    W.y_step(1)
    tok_opp()
    G.z_step(5, True)
    W.z_step(4, False)
    G.relay_step(2)
    W.y_step(2)
    G.z_step(6, True)
    W.z_step(5, False)
    G.relay_step(3)
    W.y_step(3)
    x_arrivals(oz)
    G.z_step(7, True)
    W.z_step(6, False)
    G.relay_step(4)
    W.y_step(4)
    W.z_step(7, False)
    G.relay_step(5)
    W.y_step(5)
    x_far(oz)

    @pl.loop(6, 8)
    def _(s):
        G.relay_step(s)
        W.y_step(s)

    for r in range(X):
        for q in range(2):
            wait_on(blk(1 - c, (x + r) % X, q), psem.at[1, r * 2 + q])

    TN = min(256, D)

    @pl.loop(0, D // TN)
    def _(n):
        cols = pl.ds(pl.multiple_of(n * TN, TN), TN)
        picked[:, cols] = jnp.dot(oh[...], tok[:, cols], preferred_element_type=F32).astype(BF)

    @pl.loop(0, 4)
    def _(s):
        W.relay_step(s)

    G.arrived()
    TH = min(256, H)

    @pl.loop(0, H // TH)
    def _(n):
        ga = jnp.dot(picked[...], gu[:, pl.ds(pl.multiple_of(n * TH, TH), TH)], preferred_element_type=F32)
        ub = jnp.dot(picked[...], gu[:, pl.ds(pl.multiple_of(H + n * TH, TH), TH)], preferred_element_type=F32)
        hidden[:, pl.ds(pl.multiple_of(n * TH, TH), TH)] = (ga / (1.0 + jnp.exp(-ga)) * ub).astype(BF)

    @pl.loop(4, 8)
    def _(s):
        W.relay_step(s)

    W.arrived()

    HB = 2 * X * T
    TM = min(256, HB)

    def s1(n):
        cols = pl.ds(pl.multiple_of(n * CW, CW), CW)
        o = jnp.dot(hidden[...], dn[:, cols], preferred_element_type=F32)
        contrib[...] = (gw_col[...] * o).astype(BF)

        def spread(base):
            @pl.loop(0, HB // TM)
            def _(m):
                r = pl.ds(pl.multiple_of(base + m * TM, TM), TM)
                dense[n, r, :] = jnp.dot(oht[r, :], contrib[...], preferred_element_type=F32).astype(BF)

        theirs = pl.multiple_of((1 - c) * HB, HB)
        spread(theirs)
        remote(dense.at[n, pl.ds(theirs, HB)], prcv.at[n], csem.at[n, 0], csem.at[n, 1], dev_c).start()
        spread(pl.multiple_of(c * HB, HB))

    def pblk(n, x_, q_, count=1):
        return prcv.at[n, pl.ds(pl.multiple_of((x_ * 2 + q_) * T, T), count * T)]

    def s2(n):
        wait_on(prcv.at[n], csem.at[n, 1])

        @pl.loop(0, 2 * X)
        def _(b):
            r = pl.ds(pl.multiple_of(b * T, T), T)
            mine = dense[n, pl.ds(pl.multiple_of(c * HB + b * T, T), T), :]
            prcv[n, r, :] = (prcv[n, r, :].astype(F32) + mine.astype(F32)).astype(BF)

        for d in range(2):
            remote(pblk(n, x2, d), xrl.at[d, n], csem.at[n, 2 + d], csem.at[n, 4 + d], dev_x[d]).start()

    def s3(n):
        for d, x_ in ((0, xp), (1, xm)):
            wait_on(xrl.at[d, n], csem.at[n, 4 + d])
            r = pl.ds(pl.multiple_of((x_ * 2 + d) * T, T), T)
            prcv[n, r, :] = (prcv[n, r, :].astype(F32) + xrl[d, n].astype(F32)).astype(BF)
            remote(pblk(n, x_, 0, 2), xf.at[d, n], csem.at[n, 6 + d], csem.at[n, 8 + d], dev_x[d]).start()

    def total(n, q):
        r = pl.ds(pl.multiple_of((x * 2 + q) * T, T), T)
        g = pl.ds(pl.multiple_of(q * T, T), T)
        return prcv[n, r, :].astype(F32) + xf[0, n, g, :].astype(F32) + xf[1, n, g, :].astype(F32)

    def s4(n):
        for d in range(2):
            wait_on(xf.at[d, n], csem.at[n, 8 + d])
        zsend[n] = total(n, oz).astype(BF)
        for d in range(2):
            remote(zsend.at[n, pl.ds(d * T2, T2)], zrel.at[d, n], csem.at[n, 10 + d], csem.at[n, 12 + d], dev_q[d]).start()

    def s5(n):
        for d in range(2):
            wait_on(zrel.at[d, n], csem.at[n, 12 + d])
            remote(zrel.at[d, n], zfin.at[n, pl.ds(d * T2, T2)], csem.at[n, 14 + d], csem.at[n, 16 + d], dev_q[d]).start()

    def s6(n):
        for d in range(2):
            wait_on(zfin.at[n, pl.ds(d * T2, T2)], csem.at[n, 16 + d])
        out[:, pl.ds(pl.multiple_of(n * CW, CW), CW)] = (total(n, zh) + zfin[n].astype(F32)).astype(BF)

    stages = (s1, s2, s3, s4, s5, s6)

    @pl.loop(0, NC + len(stages) - 1)
    def _(t):
        for i in reversed(range(len(stages))):
            @pl.when((t >= i) & (t < NC + i))
            def _():
                stages[i](t - i)

    G.drain()
    W.drain()
    for d in range(2):
        wait_sent_on(rz.at[d], tsem.at[0, d])
        wait_sent_on(rz.at[d], tsem.at[2, d])
    for q in range(2):
        for i in (0, 1, 4):
            wait_sent_on(tin, xsem.at[i, q])
        for r in range(X):
            wait_sent_on(tin, psem.at[0, r * 2 + q])

    @pl.loop(0, NC)
    def _(n):
        wait_sent_on(prcv.at[n], csem.at[n, 0])
        for d in range(2):
            wait_sent_on(xrl.at[d, n], csem.at[n, 2 + d])
            wait_sent_on(xf.at[d, n], csem.at[n, 6 + d])
            wait_sent_on(zrel.at[d, n], csem.at[n, 10 + d])
            wait_sent_on(zrel.at[d, n], csem.at[n, 14 + d])


def per_device(ZL, tokens, choice_rows, gate_weights, w_gate, w_up, w_down):
    T, D = tokens.shape
    H = w_gate.shape[2]
    CAP = choice_rows.shape[2]
    group = 4 * X * T
    CW = D // NC
    rows = choice_rows[0, 0]
    dev, r = rows // T, rows % T
    zh, x, c = dev // (2 * X), (dev // 2) % X, dev % 2
    rows = (c * (2 * X) + x * 2 + zh) * T + r
    gu_in = jnp.concatenate([w_gate[0], w_up[0]], axis=1)
    dn_in = w_down[0]
    dps = Y * ZL
    vmem = pl.BlockSpec(memory_space=pltpu.VMEM)
    return pl.pallas_call(
        functools.partial(layer_kernel, ZL),
        out_shape=jax.ShapeDtypeStruct((T, D), BF),
        in_specs=[vmem] * 6,
        out_specs=vmem,
        scratch_shapes=[
            pltpu.VMEM((group, D), BF),
            pltpu.VMEM((dps * gu_in.shape[0], 2 * H), BF),
            pltpu.VMEM((dps * dn_in.shape[0], D), BF),
            pltpu.VMEM((CAP, group), BF),
            pltpu.VMEM((group, CAP), BF),
            pltpu.VMEM((CAP, D), BF),
            pltpu.VMEM((CAP, H), BF),
            pltpu.VMEM((CAP, CW), BF),
            pltpu.VMEM((NC, group, CW), BF),
            pltpu.VMEM((2, T // 2, D), BF),
            pltpu.VMEM((NC, group // 2, CW), BF),
            pltpu.VMEM((2, NC, T, CW), BF),
            pltpu.VMEM((2, NC, 2 * T, CW), BF),
            pltpu.VMEM((NC, T, CW), BF),
            pltpu.VMEM((2, NC, T // 2, CW), BF),
            pltpu.VMEM((NC, T, CW), BF),
            pltpu.SemaphoreType.DMA((11, ZL)),
            pltpu.SemaphoreType.DMA((11, ZL)),
            pltpu.SemaphoreType.DMA((4, 2)),
            pltpu.SemaphoreType.DMA((6, 2)),
            pltpu.SemaphoreType.DMA((2, 8)),
            pltpu.SemaphoreType.DMA((NC, 18)),
        ],
        compiler_params=pltpu.CompilerParams(
            collective_id=0, has_side_effects=True, vmem_limit_bytes=62 * 1024 * 1024
        ),
    )(tokens, gu_in, dn_in, rows.reshape(CAP, 1), rows.reshape(1, CAP), gate_weights.reshape(CAP, 1))


def solution(mesh):
    return jax.shard_map(
        functools.partial(per_device, mesh.shape["dp"] // Y),
        mesh=mesh,
        in_specs=(
            P(("dp", "expert"), None),
            P("dp", "expert", None),
            P("dp", "expert", None),
            P("expert", "dp", None),
            P("expert", "dp", None),
            P("expert", "dp", None),
        ),
        out_specs=P(("dp", "expert"), None),
        check_vma=False,
    )
```

```python
import functools

import jax
import jax.numpy as jnp
from jax import lax
from jax.experimental import pallas as pl
from jax.experimental.pallas import tpu as pltpu
from jax.sharding import PartitionSpec as P

MESH = pl.DeviceIdType.MESH
Y = 4
X = 4
NC = 4
NP = 4
BF = jnp.bfloat16
F32 = jnp.float32


def remote(src, dst, send_sem, recv_sem, device):
    return pltpu.make_async_remote_copy(
        src_ref=src,
        dst_ref=dst,
        send_sem=send_sem,
        recv_sem=recv_sem,
        device_id=device,
        device_id_type=MESH,
    )


def layer_kernel(
    ZL,
    tin, wg_in, wu_in, dn_in, rows_ref, gw_ref,
    out,
    gw_col, tok, gu, dn, oh, oht, picked, hidden, contrib, dense,
    rz, prcv, xrl, xf, zsend, zrel, zfin,
    gsem, dsem, lsem, xsem, rsem, psem, xown, pown, csem,
):
    T, D = tin.shape
    H = gu.shape[1] // 2
    CAP = rows_ref.shape[1]
    R = wg_in.shape[0]
    CW = D // NC
    T2 = T // 2
    dp = lax.axis_index("dp")
    ex = lax.axis_index("expert")
    y, k = dp // ZL, dp % ZL
    zh, x, c = ex // (2 * X), (ex // 2) % X, ex % 2
    z = zh * ZL + k
    oz = 1 - zh
    yp, ym, y2 = (y + 1) % Y, (y + 3) % Y, (y + 2) % Y
    xp, xm, x2 = (x + 1) % X, (x + 3) % X, (x + 2) % X
    zq = ((z + ZL // 2) % (2 * ZL), (z + 2 * ZL - ZL // 2) % (2 * ZL))

    def dev(y_=y, k_=k, zh_=zh, x_=x, c_=c):
        return (y_ * ZL + k_, zh_ * (2 * X) + x_ * 2 + c_)

    dev_y = (dev(y_=yp), dev(y_=ym))
    dev_x = (dev(x_=xp), dev(x_=xm))
    dev_z = (dev(k_=k + 1), dev(k_=k - 1))
    dev_q = tuple(dev(k_=v % ZL, zh_=v // ZL) for v in zq)
    dev_c = dev(c_=1 - c)
    has_z = (k < ZL - 1, k > 0)

    own_rows = pl.ds(pl.multiple_of(dp * R, R), R)
    gu[own_rows, :H] = wg_in[...]
    gu[own_rows, H:] = wu_in[...]
    gu_own = gu.at[own_rows]

    barrier = pltpu.get_barrier_semaphore()
    for peer in dev_y + dev_x + dev_q + (dev_c,):
        pl.semaphore_signal(barrier, inc=1, device_id=peer, device_id_type=MESH)
    for d in range(2):
        @pl.when(has_z[d])
        def _():
            pl.semaphore_signal(barrier, inc=1, device_id=dev_z[d], device_id_type=MESH)
    pl.semaphore_wait(barrier, 7 + jnp.where(k < ZL - 1, 1, 0) + jnp.where(k > 0, 1, 0))

    class Part:
        def __init__(self, own, buf, sem):
            self.own, self.buf, self.sem = own, buf, sem
            self.R = own.shape[0]

        def rows(self, y_, j, half=None):
            R = self.R
            if half is None:
                return self.buf.at[pl.ds(pl.multiple_of((y_ * ZL + j) * R, R), R)]
            h = R // 2
            return self.buf.at[pl.ds(pl.multiple_of((y_ * ZL + j) * R + half * h, h), h)]

        def z_send(self, src, j, d):
            remote(src, self.rows(y, j), self.sem.at[1 + d, j], self.sem.at[0, j], dev_z[d]).start()

        def y_send(self, src, j):
            for d in range(2):
                remote(src, self.rows(y, j), self.sem.at[3 + d, j], self.sem.at[5 + d, j], dev_y[d]).start()

        def wait(self, ref, i, j):
            remote(ref, ref, self.sem.at[1, j], self.sem.at[i, j], dev_c).wait_recv()

        def wait_sent(self, ref, i, j):
            remote(ref, ref, self.sem.at[i, j], self.sem.at[0, j], dev_c).wait_send()

        def z_step(self, s, with_y):
            for d, j in ((0, k - s), (1, k + s)):
                @pl.when((j >= 0) & (j < ZL))
                def _():
                    ref = self.rows(y, j)
                    self.wait(ref, 0, j)
                    @pl.when(has_z[d])
                    def _():
                        self.z_send(ref, j, d)
                    if with_y:
                        self.y_send(ref, j)

        def y_step(self, s):
            for d, j in ((0, k - s), (1, k + s)):
                ok = (j >= 0) & (j < ZL)
                if d == 1:
                    ok = ok & (s > 0)
                @pl.when(ok)
                def _():
                    @pl.when(s > 0)
                    def _():
                        self.y_send(self.rows(y, j), j)
                    @pl.when(s == 0)
                    def _():
                        self.y_send(self.own, j)

        def relay_step(self, s):
            for d, j in ((0, k - s), (1, k + s)):
                ok = (j >= 0) & (j < ZL)
                if d == 1:
                    ok = ok & (s > 0)
                @pl.when(ok)
                def _():
                    for e, y_ in ((0, ym), (1, yp)):
                        self.wait(self.rows(y_, j), 5 + e, j)
                        half = self.rows(y_, j, e)
                        remote(half, half, self.sem.at[7 + e, j], self.sem.at[9 + e, j], dev_y[e]).start()

        def arrived(self):
            @pl.loop(0, ZL)
            def _(j):
                for e in range(2):
                    self.wait(self.rows(y2, j, e), 9 + e, j)

        def drain(self):
            @pl.loop(0, ZL)
            def _(j):
                ref = self.rows(y, j)
                for d in range(2):
                    self.wait_sent(ref, 3 + d, j)
                    self.wait_sent(self.rows(y, j, 0), 7 + d, j)
                    ok = has_z[d] & ((j <= k) if d == 0 else (j >= k))
                    @pl.when(ok)
                    def _():
                        self.wait_sent(ref, 1 + d, j)

    G = Part(gu_own, gu, gsem)
    W = Part(dn_in, dn, dsem)

    def blk(c_, x_, q_):
        b = q_ * (2 * X) + c_ * X + x_
        return tok.at[pl.ds(pl.multiple_of(b * T, T), T)]

    TP = T2 // NP

    def piece(c_, x_, q_, h, p):
        b = q_ * (2 * X) + c_ * X + x_
        return tok.at[pl.ds(pl.multiple_of(b * T + h * T2 + p * TP, TP), TP)]

    def wait_on(ref, sem):
        remote(ref, ref, sem, sem, dev_c).wait_recv()

    def wait_sent_on(ref, sem):
        remote(ref, ref, sem, sem, dev_c).wait_send()

    def half(ref, d):
        return ref.at[pl.ds(d * T2, T2)]

    def own_start():
        for d in range(2):
            remote(tin, blk(c, x, zh), xown.at[0, d], xown.at[1, d], dev_x[d]).start()
        remote(tin, blk(c, x, zh), pown.at[0, 0], pown.at[1, 0], dev_c).start()

    def own_arrivals():
        for d, r in ((0, 3), (1, 1)):
            ref = blk(c, (x + r) % X, zh)
            wait_on(ref, xown.at[1, d])
            part = half(ref, d)
            remote(part, part, xown.at[2, d], xown.at[3, d], dev_x[d]).start()
            remote(ref, ref, pown.at[0, r], pown.at[1, r], dev_c).start()

    def own_far():
        ref = blk(c, x2, zh)
        for d in range(2):
            wait_on(half(ref, d), xown.at[3, d])
        remote(ref, ref, pown.at[0, 2], pown.at[1, 2], dev_c).start()

    def leg1(p):
        for d in range(2):
            own = tin.at[pl.ds(pl.multiple_of(d * T2 + p * TP, TP), TP)]
            dst = rz.at[d, pl.ds(pl.multiple_of(p * TP, TP), TP)]
            remote(own, dst, lsem.at[0, d, p], lsem.at[1, d, p], dev_q[d]).start()

    def leg2(p):
        for d in range(2):
            mid = rz.at[d, pl.ds(pl.multiple_of(p * TP, TP), TP)]
            wait_on(mid, lsem.at[1, d, p])
            dst = piece(c, x, 1 - zq[d] // ZL, d, p)
            remote(mid, dst, lsem.at[2, d, p], lsem.at[3, d, p], dev_q[d]).start()

    def to_partner(ref, r, h, p):
        remote(ref, ref, psem.at[0, r * 2 + h, p], psem.at[1, r * 2 + h, p], dev_c).start()

    def opp_arrived(p):
        for h in range(2):
            ref = piece(c, x, oz, h, p)
            wait_on(ref, lsem.at[3, h, p])
            for d in range(2):
                remote(ref, ref, xsem.at[d, h, p], xsem.at[2 + d, h, p], dev_x[d]).start()
            to_partner(ref, 0, h, p)

    def opp_x(p):
        for d, r in ((0, 3), (1, 1)):
            for h in (d, 1 - d):
                ref = piece(c, (x + r) % X, oz, h, p)
                wait_on(ref, xsem.at[2 + d, h, p])
                if h == d:
                    remote(ref, ref, rsem.at[0, h, p], rsem.at[1, h, p], dev_x[d]).start()
                to_partner(ref, r, h, p)

    def opp_far(p):
        for h in range(2):
            ref = piece(c, x2, oz, h, p)
            wait_on(ref, rsem.at[1, h, p])
            to_partner(ref, 2, h, p)

    for d in range(2):
        @pl.when(has_z[d])
        def _():
            G.z_send(gu_own, k, d)
    G.y_send(gu_own, k)
    own_start()

    dn[pl.ds(pl.multiple_of(dp * dn_in.shape[0], dn_in.shape[0]), dn_in.shape[0]), :] = dn_in[...]
    tok[pl.ds(pl.multiple_of((zh * 2 * X + c * X + x) * T, T), T), :] = tin[...]

    NB = 2 * X * 2

    def hots():
        rows = rows_ref[...]
        lt = T.bit_length() - 1
        r = rows & (T - 1)
        core = (rows >> lt) & 1
        xx = (rows >> (lt + 1)) & (X - 1)
        hh = rows >> (lt + 3)
        rows_in = (hh * (2 * X) + core * X + xx) * T + r
        rows_out = (core * (2 * X) + xx * 2 + hh) * T + r
        rows_col = jnp.broadcast_to(rows_in, (8, CAP)).T[:, 0:1]
        gw_col[...] = jnp.broadcast_to(gw_ref[...], (8, CAP)).T[:, 0:1]

        @pl.loop(0, NB)
        def _(b):
            off = pl.multiple_of(b * T, T)
            lanes = lax.broadcasted_iota(jnp.int32, (CAP, T), 1) + b * T
            oh[:, pl.ds(off, T)] = jnp.where(rows_col == lanes, 1.0, 0.0).astype(BF)
            subs = lax.broadcasted_iota(jnp.int32, (T, CAP), 0) + b * T
            oht[pl.ds(off, T), :] = jnp.where(rows_out == subs, 1.0, 0.0).astype(BF)

    def when_in(s, lo, hi, f):
        @pl.when((s >= lo) & (s < hi))
        def _():
            f(s - lo)

    DL, A0, B0, RL = 3, 1, 2, 2

    def when_at(s, lag, f):
        v = s - (A0 + lag)

        @pl.when((v >= 0) & (v % B0 == 0) & (v // B0 < NP))
        def _():
            f(v // B0)

    def dn_start(_):
        for d in range(2):
            @pl.when(has_z[d])
            def _():
                W.z_send(dn_in, k, d)
        W.y_send(dn_in, k)

    def step(s):
        when_in(s, 1, ZL, lambda i: G.z_step(i + 1, True))
        when_at(s, 0, leg1)
        when_at(s, 1, leg2)
        when_in(s, DL, DL + 1, dn_start)
        when_in(s, DL + 1, DL + ZL, lambda i: W.z_step(i + 1, True))
        when_in(s, 1, 2, lambda i: own_arrivals())
        when_at(s, 2, opp_arrived)
        when_in(s, RL, RL + ZL, G.relay_step)
        when_in(s, 2, 3, lambda i: own_far())
        when_at(s, 3, opp_x)
        when_at(s, 4, opp_far)
        when_in(s, DL + RL, DL + RL + ZL, W.relay_step)

    TN = min(256, D)
    NT = D // TN
    HG = 2 * X * T

    def pick(n, q, first):
        cols = pl.ds(pl.multiple_of(n * TN, TN), TN)
        ks = pl.ds(pl.multiple_of(q * HG, HG), HG)
        got = jnp.dot(oh[:, ks], tok[ks, cols], preferred_element_type=F32)
        if not first:
            got = got + picked[:, cols].astype(F32)
        picked[:, cols] = got.astype(BF)

    @pl.loop(1, 2)
    def _(s):
        step(s)

    hots()

    @pl.loop(2, 6)
    def _(s):
        step(s)

    for r in range(X):
        wait_on(blk(1 - c, (x + r) % X, zh), pown.at[1, r])

    @pl.loop(0, NT)
    def _(n):
        pick(n, zh, True)

    TAIL = A0 + 3 * B0 + 5

    @pl.loop(6, TAIL)
    def _(s):
        step(s)

    @pl.loop(0, NP)
    def _(p):
        for r in range(X):
            for h in range(2):
                wait_on(piece(1 - c, (x + r) % X, oz, h, p), psem.at[1, r * 2 + h, p])

    @pl.loop(0, NT)
    def _(n):
        pick(n, oz, False)

    @pl.loop(TAIL, DL + RL + ZL)
    def _(s):
        step(s)

    G.arrived()
    TH = min(256, H)

    @pl.loop(0, H // TH)
    def _(n):
        ga = jnp.dot(picked[...], gu[:, pl.ds(pl.multiple_of(n * TH, TH), TH)], preferred_element_type=F32)
        ub = jnp.dot(picked[...], gu[:, pl.ds(pl.multiple_of(H + n * TH, TH), TH)], preferred_element_type=F32)
        hidden[:, pl.ds(pl.multiple_of(n * TH, TH), TH)] = (ga / (1.0 + jnp.exp(-ga)) * ub).astype(BF)

    W.arrived()

    HB = 2 * X * T
    TM = min(256, HB)

    def s1(n):
        cols = pl.ds(pl.multiple_of(n * CW, CW), CW)
        o = jnp.dot(hidden[...], dn[:, cols], preferred_element_type=F32)
        contrib[...] = (gw_col[...] * o).astype(BF)

        def spread(base):
            @pl.loop(0, HB // TM)
            def _(m):
                r = pl.ds(pl.multiple_of(base + m * TM, TM), TM)
                dense[n, r, :] = jnp.dot(oht[r, :], contrib[...], preferred_element_type=F32).astype(BF)

        theirs = pl.multiple_of((1 - c) * HB, HB)
        spread(theirs)
        remote(dense.at[n, pl.ds(theirs, HB)], prcv.at[n], csem.at[n, 0], csem.at[n, 1], dev_c).start()
        spread(pl.multiple_of(c * HB, HB))

    def pblk(n, x_, q_, count=1):
        return prcv.at[n, pl.ds(pl.multiple_of((x_ * 2 + q_) * T, T), count * T)]

    def s2(n):
        wait_on(prcv.at[n], csem.at[n, 1])

        @pl.loop(0, 2 * X)
        def _(b):
            r = pl.ds(pl.multiple_of(b * T, T), T)
            mine = dense[n, pl.ds(pl.multiple_of(c * HB + b * T, T), T), :]
            prcv[n, r, :] = (prcv[n, r, :].astype(F32) + mine.astype(F32)).astype(BF)

        for d in range(2):
            remote(pblk(n, x2, d), xrl.at[d, n], csem.at[n, 2 + d], csem.at[n, 4 + d], dev_x[d]).start()

    def s3(n):
        for d, x_ in ((0, xp), (1, xm)):
            wait_on(xrl.at[d, n], csem.at[n, 4 + d])
            r = pl.ds(pl.multiple_of((x_ * 2 + d) * T, T), T)
            prcv[n, r, :] = (prcv[n, r, :].astype(F32) + xrl[d, n].astype(F32)).astype(BF)
            remote(pblk(n, x_, 0, 2), xf.at[d, n], csem.at[n, 6 + d], csem.at[n, 8 + d], dev_x[d]).start()

    def total(n, q):
        r = pl.ds(pl.multiple_of((x * 2 + q) * T, T), T)
        g = pl.ds(pl.multiple_of(q * T, T), T)
        return prcv[n, r, :].astype(F32) + xf[0, n, g, :].astype(F32) + xf[1, n, g, :].astype(F32)

    def s4(n):
        for d in range(2):
            wait_on(xf.at[d, n], csem.at[n, 8 + d])
        zsend[n] = total(n, oz).astype(BF)
        for d in range(2):
            remote(zsend.at[n, pl.ds(d * T2, T2)], zrel.at[d, n], csem.at[n, 10 + d], csem.at[n, 12 + d], dev_q[d]).start()

    def s5(n):
        for d in range(2):
            wait_on(zrel.at[d, n], csem.at[n, 12 + d])
            remote(zrel.at[d, n], zfin.at[n, pl.ds(d * T2, T2)], csem.at[n, 14 + d], csem.at[n, 16 + d], dev_q[d]).start()

    def s6(n):
        for d in range(2):
            wait_on(zfin.at[n, pl.ds(d * T2, T2)], csem.at[n, 16 + d])
        out[:, pl.ds(pl.multiple_of(n * CW, CW), CW)] = (total(n, zh) + zfin[n].astype(F32)).astype(BF)

    stages = (s1, s2, s3, s4, s5, s6)

    @pl.loop(0, NC + len(stages) - 1)
    def _(t):
        for i in reversed(range(len(stages))):
            @pl.when((t >= i) & (t < NC + i))
            def _():
                stages[i](t - i)

    G.drain()
    W.drain()
    for d in range(2):
        wait_sent_on(tin, xown.at[0, d])
        wait_sent_on(half(tin, d), xown.at[2, d])
    for r in range(X):
        wait_sent_on(tin, pown.at[0, r])

    @pl.loop(0, NP)
    def _(p):
        ref = tin.at[pl.ds(0, TP)]
        for h in range(2):
            wait_sent_on(ref, lsem.at[0, h, p])
            wait_sent_on(ref, lsem.at[2, h, p])
            wait_sent_on(ref, xsem.at[0, h, p])
            wait_sent_on(ref, xsem.at[1, h, p])
            wait_sent_on(ref, rsem.at[0, h, p])
            for r in range(X):
                wait_sent_on(ref, psem.at[0, r * 2 + h, p])

    @pl.loop(0, NC)
    def _(n):
        wait_sent_on(prcv.at[n], csem.at[n, 0])
        for d in range(2):
            wait_sent_on(xrl.at[d, n], csem.at[n, 2 + d])
            wait_sent_on(xf.at[d, n], csem.at[n, 6 + d])
            wait_sent_on(zrel.at[d, n], csem.at[n, 10 + d])
            wait_sent_on(zrel.at[d, n], csem.at[n, 14 + d])


def per_device(ZL, tokens, choice_rows, gate_weights, w_gate, w_up, w_down):
    T, D = tokens.shape
    H = w_gate.shape[2]
    CAP = choice_rows.shape[2]
    group = 4 * X * T
    CW = D // NC
    K = w_gate.shape[1]
    dn_in = w_down[0]
    dps = Y * ZL
    vmem = pl.BlockSpec(memory_space=pltpu.VMEM)
    return pl.pallas_call(
        functools.partial(layer_kernel, ZL),
        out_shape=jax.ShapeDtypeStruct((T, D), BF),
        in_specs=[vmem] * 6,
        out_specs=vmem,
        scratch_shapes=[
            pltpu.VMEM((CAP, 1), F32),
            pltpu.VMEM((group, D), BF),
            pltpu.VMEM((dps * K, 2 * H), BF),
            pltpu.VMEM((dps * dn_in.shape[0], D), BF),
            pltpu.VMEM((CAP, group), BF),
            pltpu.VMEM((group, CAP), BF),
            pltpu.VMEM((CAP, D), BF),
            pltpu.VMEM((CAP, H), BF),
            pltpu.VMEM((CAP, CW), BF),
            pltpu.VMEM((NC, group, CW), BF),
            pltpu.VMEM((2, T // 2, D), BF),
            pltpu.VMEM((NC, group // 2, CW), BF),
            pltpu.VMEM((2, NC, T, CW), BF),
            pltpu.VMEM((2, NC, 2 * T, CW), BF),
            pltpu.VMEM((NC, T, CW), BF),
            pltpu.VMEM((2, NC, T // 2, CW), BF),
            pltpu.VMEM((NC, T, CW), BF),
            pltpu.SemaphoreType.DMA((11, ZL)),
            pltpu.SemaphoreType.DMA((11, ZL)),
            pltpu.SemaphoreType.DMA((4, 2, NP)),
            pltpu.SemaphoreType.DMA((4, 2, NP)),
            pltpu.SemaphoreType.DMA((2, 2, NP)),
            pltpu.SemaphoreType.DMA((2, 2 * X, NP)),
            pltpu.SemaphoreType.DMA((4, 2)),
            pltpu.SemaphoreType.DMA((2, X)),
            pltpu.SemaphoreType.DMA((NC, 18)),
        ],
        compiler_params=pltpu.CompilerParams(
            collective_id=0, has_side_effects=True, vmem_limit_bytes=62 * 1024 * 1024
        ),
    )(tokens, w_gate[0], w_up[0], dn_in, choice_rows[0], gate_weights[0])


def solution(mesh):
    return jax.shard_map(
        functools.partial(per_device, mesh.shape["dp"] // Y),
        mesh=mesh,
        in_specs=(
            P(("dp", "expert"), None),
            P("dp", "expert", None),
            P("dp", "expert", None),
            P("expert", "dp", None),
            P("expert", "dp", None),
            P("expert", "dp", None),
        ),
        out_specs=P(("dp", "expert"), None),
        check_vma=False,
    )
```

```python
import functools

import jax
import jax.numpy as jnp
from jax import lax
from jax.experimental import pallas as pl
from jax.experimental.pallas import tpu as pltpu
from jax.sharding import PartitionSpec as P

MESH = pl.DeviceIdType.MESH
Y = 4
X = 4
NC = 8
LAGS = (0, 1, 2, 3, 5, 7)
NP = 4
BF = jnp.bfloat16
F32 = jnp.float32


def remote(src, dst, send_sem, recv_sem, device):
    return pltpu.make_async_remote_copy(
        src_ref=src,
        dst_ref=dst,
        send_sem=send_sem,
        recv_sem=recv_sem,
        device_id=device,
        device_id_type=MESH,
    )


def layer_kernel(
    ZL,
    tin, wg_in, wu_in, dn_in, rows_ref, gw_ref,
    out,
    gw_col, tok, gu, dn, oh, oht, picked, hidden, contrib, dense,
    rz, prcv, xrl, xf, zsend, zrel, zfin,
    gsem, dsem0, dsem1, lsem, xsem, rsem, psem, xown, pown, csem,
):
    T, D = tin.shape
    H = gu.shape[1] // 2
    CAP = rows_ref.shape[1]
    R = wg_in.shape[0]
    CW = D // NC
    T2 = T // 2
    dp = lax.axis_index("dp")
    ex = lax.axis_index("expert")
    y, k = dp // ZL, dp % ZL
    zh, x, c = ex // (2 * X), (ex // 2) % X, ex % 2
    z = zh * ZL + k
    oz = 1 - zh
    yp, ym, y2 = (y + 1) % Y, (y + 3) % Y, (y + 2) % Y
    xp, xm, x2 = (x + 1) % X, (x + 3) % X, (x + 2) % X
    zq = ((z + ZL // 2) % (2 * ZL), (z + 2 * ZL - ZL // 2) % (2 * ZL))

    def dev(y_=y, k_=k, zh_=zh, x_=x, c_=c):
        return (y_ * ZL + k_, zh_ * (2 * X) + x_ * 2 + c_)

    dev_y = (dev(y_=yp), dev(y_=ym))
    dev_x = (dev(x_=xp), dev(x_=xm))
    dev_z = (dev(k_=k + 1), dev(k_=k - 1))
    dev_q = tuple(dev(k_=v % ZL, zh_=v // ZL) for v in zq)
    dev_c = dev(c_=1 - c)
    has_z = (k < ZL - 1, k > 0)

    own_rows = pl.ds(pl.multiple_of(dp * R, R), R)
    gu[own_rows, :H] = wg_in[...]
    gu[own_rows, H:] = wu_in[...]
    gu_own = gu.at[own_rows]

    barrier = pltpu.get_barrier_semaphore()
    for peer in dev_y + dev_x + dev_q + (dev_c,):
        pl.semaphore_signal(barrier, inc=1, device_id=peer, device_id_type=MESH)
    for d in range(2):
        @pl.when(has_z[d])
        def _():
            pl.semaphore_signal(barrier, inc=1, device_id=dev_z[d], device_id_type=MESH)
    pl.semaphore_wait(barrier, 7 + jnp.where(k < ZL - 1, 1, 0) + jnp.where(k > 0, 1, 0))

    class Part:
        def __init__(self, own, buf, sem):
            self.own, self.buf, self.sem = own, buf, sem
            self.R = own.shape[0]

        def rows(self, y_, j, half=None):
            R = self.R
            if half is None:
                return self.buf.at[pl.ds(pl.multiple_of((y_ * ZL + j) * R, R), R)]
            h = R // 2
            return self.buf.at[pl.ds(pl.multiple_of((y_ * ZL + j) * R + half * h, h), h)]

        def z_send(self, src, j, d):
            remote(src, self.rows(y, j), self.sem.at[1 + d, j], self.sem.at[0, j], dev_z[d]).start()

        def y_send(self, src, j):
            for d in range(2):
                remote(src, self.rows(y, j), self.sem.at[3 + d, j], self.sem.at[5 + d, j], dev_y[d]).start()

        def wait(self, ref, i, j):
            remote(ref, ref, self.sem.at[1, j], self.sem.at[i, j], dev_c).wait_recv()

        def wait_sent(self, ref, i, j):
            remote(ref, ref, self.sem.at[i, j], self.sem.at[0, j], dev_c).wait_send()

        def z_step(self, s, with_y):
            for d, j in ((0, k - s), (1, k + s)):
                @pl.when((j >= 0) & (j < ZL))
                def _():
                    ref = self.rows(y, j)
                    self.wait(ref, 0, j)
                    @pl.when(has_z[d])
                    def _():
                        self.z_send(ref, j, d)
                    if with_y:
                        self.y_send(ref, j)

        def y_step(self, s):
            for d, j in ((0, k - s), (1, k + s)):
                ok = (j >= 0) & (j < ZL)
                if d == 1:
                    ok = ok & (s > 0)
                @pl.when(ok)
                def _():
                    @pl.when(s > 0)
                    def _():
                        self.y_send(self.rows(y, j), j)
                    @pl.when(s == 0)
                    def _():
                        self.y_send(self.own, j)

        def relay_step(self, s):
            for d, j in ((0, k - s), (1, k + s)):
                ok = (j >= 0) & (j < ZL)
                if d == 1:
                    ok = ok & (s > 0)
                @pl.when(ok)
                def _():
                    for e, y_ in ((0, ym), (1, yp)):
                        self.wait(self.rows(y_, j), 5 + e, j)
                        half = self.rows(y_, j, e)
                        remote(half, half, self.sem.at[7 + e, j], self.sem.at[9 + e, j], dev_y[e]).start()

        def arrived(self):
            @pl.loop(0, ZL)
            def _(j):
                for e in range(2):
                    self.wait(self.rows(y2, j, e), 9 + e, j)

        def drain(self):
            @pl.loop(0, ZL)
            def _(j):
                ref = self.rows(y, j)
                for d in range(2):
                    self.wait_sent(ref, 3 + d, j)
                    self.wait_sent(self.rows(y, j, 0), 7 + d, j)
                    ok = has_z[d] & ((j <= k) if d == 0 else (j >= k))
                    @pl.when(ok)
                    def _():
                        self.wait_sent(ref, 1 + d, j)

    G = Part(gu_own, gu, gsem)
    D2 = D // 2
    WS = tuple(Part(dn_in.at[:, pl.ds(i * D2, D2)], dn.at[i], m) for i, m in enumerate((dsem0, dsem1)))

    def blk(c_, x_, q_):
        b = q_ * (2 * X) + c_ * X + x_
        return tok.at[pl.ds(pl.multiple_of(b * T, T), T)]

    TP = T2 // NP

    def piece(c_, x_, q_, h, p):
        b = q_ * (2 * X) + c_ * X + x_
        return tok.at[pl.ds(pl.multiple_of(b * T + h * T2 + p * TP, TP), TP)]

    def wait_on(ref, sem):
        remote(ref, ref, sem, sem, dev_c).wait_recv()

    def wait_sent_on(ref, sem):
        remote(ref, ref, sem, sem, dev_c).wait_send()

    def half(ref, d):
        return ref.at[pl.ds(d * T2, T2)]

    def own_start():
        for d in range(2):
            remote(tin, blk(c, x, zh), xown.at[0, d], xown.at[1, d], dev_x[d]).start()
        remote(tin, blk(c, x, zh), pown.at[0, 0], pown.at[1, 0], dev_c).start()

    def own_arrivals():
        for d, r in ((0, 3), (1, 1)):
            ref = blk(c, (x + r) % X, zh)
            wait_on(ref, xown.at[1, d])
            part = half(ref, d)
            remote(part, part, xown.at[2, d], xown.at[3, d], dev_x[d]).start()
            remote(ref, ref, pown.at[0, r], pown.at[1, r], dev_c).start()

    def own_far():
        ref = blk(c, x2, zh)
        for d in range(2):
            wait_on(half(ref, d), xown.at[3, d])
        remote(ref, ref, pown.at[0, 2], pown.at[1, 2], dev_c).start()

    def leg1(p):
        for d in range(2):
            own = tin.at[pl.ds(pl.multiple_of(d * T2 + p * TP, TP), TP)]
            dst = rz.at[d, pl.ds(pl.multiple_of(p * TP, TP), TP)]
            remote(own, dst, lsem.at[0, d, p], lsem.at[1, d, p], dev_q[d]).start()

    def leg2(p):
        for d in range(2):
            mid = rz.at[d, pl.ds(pl.multiple_of(p * TP, TP), TP)]
            wait_on(mid, lsem.at[1, d, p])
            dst = piece(c, x, 1 - zq[d] // ZL, d, p)
            remote(mid, dst, lsem.at[2, d, p], lsem.at[3, d, p], dev_q[d]).start()

    def to_partner(ref, r, h, p):
        remote(ref, ref, psem.at[0, r * 2 + h, p], psem.at[1, r * 2 + h, p], dev_c).start()

    def opp_arrived(p):
        for h in range(2):
            ref = piece(c, x, oz, h, p)
            wait_on(ref, lsem.at[3, h, p])
            for d in range(2):
                remote(ref, ref, xsem.at[d, h, p], xsem.at[2 + d, h, p], dev_x[d]).start()
            to_partner(ref, 0, h, p)

    def opp_x(p):
        for d, r in ((0, 3), (1, 1)):
            for h in (d, 1 - d):
                ref = piece(c, (x + r) % X, oz, h, p)
                wait_on(ref, xsem.at[2 + d, h, p])
                if h == d:
                    remote(ref, ref, rsem.at[0, h, p], rsem.at[1, h, p], dev_x[d]).start()
                to_partner(ref, r, h, p)

    def opp_far(p):
        for h in range(2):
            ref = piece(c, x2, oz, h, p)
            wait_on(ref, rsem.at[1, h, p])
            to_partner(ref, 2, h, p)

    for d in range(2):
        @pl.when(has_z[d])
        def _():
            G.z_send(gu_own, k, d)
    G.y_send(gu_own, k)
    own_start()

    for i in range(2):
        dn[i, pl.ds(pl.multiple_of(dp * dn_in.shape[0], dn_in.shape[0]), dn_in.shape[0]), :] = dn_in[:, i * D2 : (i + 1) * D2]
    tok[pl.ds(pl.multiple_of((zh * 2 * X + c * X + x) * T, T), T), :] = tin[...]

    NB = 2 * X * 2

    def hots():
        rows = rows_ref[...]
        lt = T.bit_length() - 1
        r = rows & (T - 1)
        core = (rows >> lt) & 1
        xx = (rows >> (lt + 1)) & (X - 1)
        hh = rows >> (lt + 3)
        rows_in = (hh * (2 * X) + core * X + xx) * T + r
        rows_out = (core * (2 * X) + xx * 2 + hh) * T + r
        rows_col = jnp.broadcast_to(rows_in, (8, CAP)).T[:, 0:1]
        gw_col[...] = jnp.broadcast_to(gw_ref[...], (8, CAP)).T[:, 0:1]

        @pl.loop(0, NB)
        def _(b):
            off = pl.multiple_of(b * T, T)
            lanes = lax.broadcasted_iota(jnp.int32, (CAP, T), 1) + b * T
            oh[:, pl.ds(off, T)] = jnp.where(rows_col == lanes, 1.0, 0.0).astype(BF)
            subs = lax.broadcasted_iota(jnp.int32, (T, CAP), 0) + b * T
            oht[pl.ds(off, T), :] = jnp.where(rows_out == subs, 1.0, 0.0).astype(BF)

    def when_in(s, lo, hi, f):
        @pl.when((s >= lo) & (s < hi))
        def _():
            f(s - lo)

    D1 = 3
    DL, A0, B0, RL = 3, 1, 2, 2

    def when_at(s, lag, f):
        v = s - (A0 + lag)

        @pl.when((v >= 0) & (v % B0 == 0) & (v // B0 < NP))
        def _():
            f(v // B0)

    def dn_step(W, s, lag):
        @pl.when(s == lag)
        def _():
            for d in range(2):
                @pl.when(has_z[d])
                def _():
                    W.z_send(W.own, k, d)
            W.y_send(W.own, k)

        when_in(s, lag + 1, lag + ZL, lambda i: W.z_step(i + 1, True))
        when_in(s, lag + RL, lag + RL + ZL, W.relay_step)

    def step(s):
        when_in(s, 1, ZL, lambda i: G.z_step(i + 1, True))
        when_at(s, 0, leg1)
        when_at(s, 1, leg2)
        when_in(s, 1, 2, lambda i: own_arrivals())
        when_at(s, 2, opp_arrived)
        when_in(s, RL, RL + ZL, G.relay_step)
        when_in(s, 2, 3, lambda i: own_far())
        when_at(s, 3, opp_x)
        when_at(s, 4, opp_far)
        dn_step(WS[0], s, DL)
        dn_step(WS[1], s, DL + D1)

    TN = min(256, D)
    NT = D // TN
    HG = 2 * X * T

    def pick(n, q, first):
        cols = pl.ds(pl.multiple_of(n * TN, TN), TN)
        ks = pl.ds(pl.multiple_of(q * HG, HG), HG)
        got = jnp.dot(oh[:, ks], tok[ks, cols], preferred_element_type=F32)
        if not first:
            got = got + picked[:, cols].astype(F32)
        picked[:, cols] = got.astype(BF)

    @pl.loop(1, 2)
    def _(s):
        step(s)

    hots()

    @pl.loop(2, 6)
    def _(s):
        step(s)

    for r in range(X):
        wait_on(blk(1 - c, (x + r) % X, zh), pown.at[1, r])

    @pl.loop(0, NT)
    def _(n):
        pick(n, zh, True)

    TAIL = A0 + 3 * B0 + 5
    END = DL + RL + ZL

    @pl.loop(6, TAIL)
    def _(s):
        step(s)

    @pl.loop(0, NP)
    def _(p):
        for r in range(X):
            for h in range(2):
                wait_on(piece(1 - c, (x + r) % X, oz, h, p), psem.at[1, r * 2 + h, p])

    @pl.loop(0, NT)
    def _(n):
        pick(n, oz, False)

    @pl.loop(TAIL, max(END, TAIL))
    def _(s):
        step(s)

    G.arrived()
    TH = min(256, H)

    @pl.loop(0, H // TH)
    def _(n):
        ga = jnp.dot(picked[...], gu[:, pl.ds(pl.multiple_of(n * TH, TH), TH)], preferred_element_type=F32)
        ub = jnp.dot(picked[...], gu[:, pl.ds(pl.multiple_of(H + n * TH, TH), TH)], preferred_element_type=F32)
        hidden[:, pl.ds(pl.multiple_of(n * TH, TH), TH)] = (ga / (1.0 + jnp.exp(-ga)) * ub).astype(BF)

    WS[0].arrived()

    HB = 2 * X * T
    TM = min(256, HB)

    def s1(n):
        cols2 = pl.ds(pl.multiple_of((n % (NC // 2)) * CW, CW), CW)
        o = jnp.dot(hidden[...], dn[n // (NC // 2), :, cols2], preferred_element_type=F32)
        contrib[...] = (gw_col[...] * o).astype(BF)

        def spread(base):
            @pl.loop(0, HB // TM)
            def _(m):
                r = pl.ds(pl.multiple_of(base + m * TM, TM), TM)
                dense[n, r, :] = jnp.dot(oht[r, :], contrib[...], preferred_element_type=F32).astype(BF)

        theirs = pl.multiple_of((1 - c) * HB, HB)
        spread(theirs)
        remote(dense.at[n, pl.ds(theirs, HB)], prcv.at[n], csem.at[n, 0], csem.at[n, 1], dev_c).start()
        spread(pl.multiple_of(c * HB, HB))

    def pblk(n, x_, q_, count=1):
        return prcv.at[n, pl.ds(pl.multiple_of((x_ * 2 + q_) * T, T), count * T)]

    def s2(n):
        wait_on(prcv.at[n], csem.at[n, 1])

        @pl.loop(0, 2 * X)
        def _(b):
            r = pl.ds(pl.multiple_of(b * T, T), T)
            mine = dense[n, pl.ds(pl.multiple_of(c * HB + b * T, T), T), :]
            prcv[n, r, :] = (prcv[n, r, :].astype(F32) + mine.astype(F32)).astype(BF)

        for d in range(2):
            remote(pblk(n, x2, d), xrl.at[d, n], csem.at[n, 2 + d], csem.at[n, 4 + d], dev_x[d]).start()

    def s3(n):
        for d, x_ in ((0, xp), (1, xm)):
            wait_on(xrl.at[d, n], csem.at[n, 4 + d])
            r = pl.ds(pl.multiple_of((x_ * 2 + d) * T, T), T)
            prcv[n, r, :] = (prcv[n, r, :].astype(F32) + xrl[d, n].astype(F32)).astype(BF)
            remote(pblk(n, x_, 0, 2), xf.at[d, n], csem.at[n, 6 + d], csem.at[n, 8 + d], dev_x[d]).start()

    def total(n, q):
        r = pl.ds(pl.multiple_of((x * 2 + q) * T, T), T)
        g = pl.ds(pl.multiple_of(q * T, T), T)
        return prcv[n, r, :].astype(F32) + xf[0, n, g, :].astype(F32) + xf[1, n, g, :].astype(F32)

    def s4(n):
        for d in range(2):
            wait_on(xf.at[d, n], csem.at[n, 8 + d])
        zsend[n] = total(n, oz).astype(BF)
        for d in range(2):
            remote(zsend.at[n, pl.ds(d * T2, T2)], zrel.at[d, n], csem.at[n, 10 + d], csem.at[n, 12 + d], dev_q[d]).start()

    def s5(n):
        for d in range(2):
            wait_on(zrel.at[d, n], csem.at[n, 12 + d])
            remote(zrel.at[d, n], zfin.at[n, pl.ds(d * T2, T2)], csem.at[n, 14 + d], csem.at[n, 16 + d], dev_q[d]).start()

    def s6(n):
        for d in range(2):
            wait_on(zfin.at[n, pl.ds(d * T2, T2)], csem.at[n, 16 + d])
        out[:, pl.ds(pl.multiple_of(n * CW, CW), CW)] = (total(n, zh) + zfin[n].astype(F32)).astype(BF)

    stages = (s1, s2, s3, s4, s5, s6)

    BEG = max(END, TAIL)

    @pl.loop(0, NC + LAGS[-1])
    def _(t):
        @pl.when(t < D1)
        def _():
            dn_step(WS[1], t + BEG, DL + D1)

        @pl.when(t == NC // 2)
        def _():
            WS[1].arrived()

        for i in reversed(range(len(stages))):
            @pl.when((t >= LAGS[i]) & (t < NC + LAGS[i]))
            def _():
                stages[i](t - LAGS[i])

    G.drain()
    WS[0].drain()
    WS[1].drain()
    for d in range(2):
        wait_sent_on(tin, xown.at[0, d])
        wait_sent_on(half(tin, d), xown.at[2, d])
    for r in range(X):
        wait_sent_on(tin, pown.at[0, r])

    @pl.loop(0, NP)
    def _(p):
        ref = tin.at[pl.ds(0, TP)]
        for h in range(2):
            wait_sent_on(ref, lsem.at[0, h, p])
            wait_sent_on(ref, lsem.at[2, h, p])
            wait_sent_on(ref, xsem.at[0, h, p])
            wait_sent_on(ref, xsem.at[1, h, p])
            wait_sent_on(ref, rsem.at[0, h, p])
            for r in range(X):
                wait_sent_on(ref, psem.at[0, r * 2 + h, p])

    @pl.loop(0, NC)
    def _(n):
        wait_sent_on(prcv.at[n], csem.at[n, 0])
        for d in range(2):
            wait_sent_on(xrl.at[d, n], csem.at[n, 2 + d])
            wait_sent_on(xf.at[d, n], csem.at[n, 6 + d])
            wait_sent_on(zrel.at[d, n], csem.at[n, 10 + d])
            wait_sent_on(zrel.at[d, n], csem.at[n, 14 + d])


def per_device(ZL, tokens, choice_rows, gate_weights, w_gate, w_up, w_down):
    T, D = tokens.shape
    H = w_gate.shape[2]
    CAP = choice_rows.shape[2]
    group = 4 * X * T
    CW = D // NC
    K = w_gate.shape[1]
    dn_in = w_down[0]
    dps = Y * ZL
    vmem = pl.BlockSpec(memory_space=pltpu.VMEM)
    return pl.pallas_call(
        functools.partial(layer_kernel, ZL),
        out_shape=jax.ShapeDtypeStruct((T, D), BF),
        in_specs=[vmem] * 6,
        out_specs=vmem,
        scratch_shapes=[
            pltpu.VMEM((CAP, 1), F32),
            pltpu.VMEM((group, D), BF),
            pltpu.VMEM((dps * K, 2 * H), BF),
            pltpu.VMEM((2, dps * dn_in.shape[0], D // 2), BF),
            pltpu.VMEM((CAP, group), BF),
            pltpu.VMEM((group, CAP), BF),
            pltpu.VMEM((CAP, D), BF),
            pltpu.VMEM((CAP, H), BF),
            pltpu.VMEM((CAP, CW), BF),
            pltpu.VMEM((NC, group, CW), BF),
            pltpu.VMEM((2, T // 2, D), BF),
            pltpu.VMEM((NC, group // 2, CW), BF),
            pltpu.VMEM((2, NC, T, CW), BF),
            pltpu.VMEM((2, NC, 2 * T, CW), BF),
            pltpu.VMEM((NC, T, CW), BF),
            pltpu.VMEM((2, NC, T // 2, CW), BF),
            pltpu.VMEM((NC, T, CW), BF),
            pltpu.SemaphoreType.DMA((11, ZL)),
            pltpu.SemaphoreType.DMA((11, ZL)),
            pltpu.SemaphoreType.DMA((11, ZL)),
            pltpu.SemaphoreType.DMA((4, 2, NP)),
            pltpu.SemaphoreType.DMA((4, 2, NP)),
            pltpu.SemaphoreType.DMA((2, 2, NP)),
            pltpu.SemaphoreType.DMA((2, 2 * X, NP)),
            pltpu.SemaphoreType.DMA((4, 2)),
            pltpu.SemaphoreType.DMA((2, X)),
            pltpu.SemaphoreType.DMA((NC, 18)),
        ],
        compiler_params=pltpu.CompilerParams(
            collective_id=0, has_side_effects=True, vmem_limit_bytes=62 * 1024 * 1024
        ),
    )(tokens, w_gate[0], w_up[0], dn_in, choice_rows[0], gate_weights[0])


def solution(mesh):
    return jax.shard_map(
        functools.partial(per_device, mesh.shape["dp"] // Y),
        mesh=mesh,
        in_specs=(
            P(("dp", "expert"), None),
            P("dp", "expert", None),
            P("dp", "expert", None),
            P("expert", "dp", None),
            P("expert", "dp", None),
            P("expert", "dp", None),
        ),
        out_specs=P(("dp", "expert"), None),
        check_vma=False,
    )
```

```python
import functools

import jax
import jax.numpy as jnp
from jax import lax
from jax.experimental import pallas as pl
from jax.experimental.pallas import tpu as pltpu
from jax.sharding import PartitionSpec as P

MESH = pl.DeviceIdType.MESH
Y = 4
X = 4
NC = 8
LAGS = (0, 1, 2, 3, 5, 7)
NP = 4
BF = jnp.bfloat16
F32 = jnp.float32


def remote(src, dst, send_sem, recv_sem, device):
    return pltpu.make_async_remote_copy(
        src_ref=src,
        dst_ref=dst,
        send_sem=send_sem,
        recv_sem=recv_sem,
        device_id=device,
        device_id_type=MESH,
    )


def layer_kernel(
    ZL,
    tin, wg_in, wu_in, dn_in, rows_ref, gw_ref,
    out,
    gw_col, tok, gu, dn, oh, oht, picked, hidden, contrib, dense,
    rz, prcv, xrl, xf, zsend, zrel, zfin,
    gsem, dsem0, dsem1, lsem, xsem, rsem, psem, xown, pown, csem,
):
    T, D = tin.shape
    H = gu.shape[1] // 2
    CAP = rows_ref.shape[1]
    R = wg_in.shape[0]
    CW = D // NC
    T2 = T // 2
    dp = lax.axis_index("dp")
    ex = lax.axis_index("expert")
    y, k = dp // ZL, dp % ZL
    zh, x, c = ex // (2 * X), (ex // 2) % X, ex % 2
    z = zh * ZL + k
    oz = 1 - zh
    yp, ym, y2 = (y + 1) % Y, (y + 3) % Y, (y + 2) % Y
    xp, xm, x2 = (x + 1) % X, (x + 3) % X, (x + 2) % X
    zq = ((z + ZL // 2) % (2 * ZL), (z + 2 * ZL - ZL // 2) % (2 * ZL))

    def dev(y_=y, k_=k, zh_=zh, x_=x, c_=c):
        return (y_ * ZL + k_, zh_ * (2 * X) + x_ * 2 + c_)

    dev_y = (dev(y_=yp), dev(y_=ym))
    dev_x = (dev(x_=xp), dev(x_=xm))
    dev_z = (dev(k_=k + 1), dev(k_=k - 1))
    dev_q = tuple(dev(k_=v % ZL, zh_=v // ZL) for v in zq)
    dev_c = dev(c_=1 - c)
    has_z = (k < ZL - 1, k > 0)

    own_rows = pl.ds(pl.multiple_of(dp * R, R), R)
    gu[own_rows, :H] = wg_in[...]
    gu[own_rows, H:] = wu_in[...]
    gu_own = gu.at[own_rows]

    barrier = pltpu.get_barrier_semaphore()
    for peer in dev_y + dev_x + dev_q + (dev_c,):
        pl.semaphore_signal(barrier, inc=1, device_id=peer, device_id_type=MESH)
    for d in range(2):
        @pl.when(has_z[d])
        def _():
            pl.semaphore_signal(barrier, inc=1, device_id=dev_z[d], device_id_type=MESH)
    pl.semaphore_wait(barrier, 7 + jnp.where(k < ZL - 1, 1, 0) + jnp.where(k > 0, 1, 0))

    class Part:
        def __init__(self, own, buf, sem):
            self.own, self.buf, self.sem = own, buf, sem
            self.R = own.shape[0]

        def rows(self, y_, j, half=None):
            R = self.R
            if half is None:
                return self.buf.at[pl.ds(pl.multiple_of((y_ * ZL + j) * R, R), R)]
            h = R // 2
            return self.buf.at[pl.ds(pl.multiple_of((y_ * ZL + j) * R + half * h, h), h)]

        def z_send(self, src, j, d):
            remote(src, self.rows(y, j), self.sem.at[1 + d, j], self.sem.at[0, j], dev_z[d]).start()

        def y_send(self, src, j):
            for d in range(2):
                remote(src, self.rows(y, j), self.sem.at[3 + d, j], self.sem.at[5 + d, j], dev_y[d]).start()

        def wait(self, ref, i, j):
            remote(ref, ref, self.sem.at[1, j], self.sem.at[i, j], dev_c).wait_recv()

        def wait_sent(self, ref, i, j):
            remote(ref, ref, self.sem.at[i, j], self.sem.at[0, j], dev_c).wait_send()

        def z_step(self, s, with_y):
            for d, j in ((0, k - s), (1, k + s)):
                @pl.when((j >= 0) & (j < ZL))
                def _():
                    ref = self.rows(y, j)
                    self.wait(ref, 0, j)
                    @pl.when(has_z[d])
                    def _():
                        self.z_send(ref, j, d)
                    if with_y:
                        self.y_send(ref, j)

        def y_step(self, s):
            for d, j in ((0, k - s), (1, k + s)):
                ok = (j >= 0) & (j < ZL)
                if d == 1:
                    ok = ok & (s > 0)
                @pl.when(ok)
                def _():
                    @pl.when(s > 0)
                    def _():
                        self.y_send(self.rows(y, j), j)
                    @pl.when(s == 0)
                    def _():
                        self.y_send(self.own, j)

        def relay_step(self, s):
            for d, j in ((0, k - s), (1, k + s)):
                ok = (j >= 0) & (j < ZL)
                if d == 1:
                    ok = ok & (s > 0)
                @pl.when(ok)
                def _():
                    for e, y_ in ((0, ym), (1, yp)):
                        self.wait(self.rows(y_, j), 5 + e, j)
                        half = self.rows(y_, j, e)
                        remote(half, half, self.sem.at[7 + e, j], self.sem.at[9 + e, j], dev_y[e]).start()

        def arrived(self):
            @pl.loop(0, ZL)
            def _(j):
                for e in range(2):
                    self.wait(self.rows(y2, j, e), 9 + e, j)

        def drain(self):
            @pl.loop(0, ZL)
            def _(j):
                ref = self.rows(y, j)
                for d in range(2):
                    self.wait_sent(ref, 3 + d, j)
                    self.wait_sent(self.rows(y, j, 0), 7 + d, j)
                    ok = has_z[d] & ((j <= k) if d == 0 else (j >= k))
                    @pl.when(ok)
                    def _():
                        self.wait_sent(ref, 1 + d, j)

    G = Part(gu_own, gu, gsem)
    D2 = D // 2
    WS = tuple(Part(dn_in.at[:, pl.ds(i * D2, D2)], dn.at[i], m) for i, m in enumerate((dsem0, dsem1)))

    def blk(c_, x_, q_):
        b = q_ * (2 * X) + c_ * X + x_
        return tok.at[pl.ds(pl.multiple_of(b * T, T), T)]

    TP = T2 // NP

    def piece(c_, x_, q_, h, p):
        b = q_ * (2 * X) + c_ * X + x_
        return tok.at[pl.ds(pl.multiple_of(b * T + h * T2 + p * TP, TP), TP)]

    def wait_on(ref, sem):
        remote(ref, ref, sem, sem, dev_c).wait_recv()

    def wait_sent_on(ref, sem):
        remote(ref, ref, sem, sem, dev_c).wait_send()

    def half(ref, d):
        return ref.at[pl.ds(d * T2, T2)]

    def own_start():
        for d in range(2):
            remote(tin, blk(c, x, zh), xown.at[0, d], xown.at[1, d], dev_x[d]).start()
        remote(tin, blk(c, x, zh), pown.at[0, 0], pown.at[1, 0], dev_c).start()

    def own_arrivals():
        for d, r in ((0, 3), (1, 1)):
            ref = blk(c, (x + r) % X, zh)
            wait_on(ref, xown.at[1, d])
            part = half(ref, d)
            remote(part, part, xown.at[2, d], xown.at[3, d], dev_x[d]).start()
            remote(ref, ref, pown.at[0, r], pown.at[1, r], dev_c).start()

    def own_far():
        ref = blk(c, x2, zh)
        for d in range(2):
            wait_on(half(ref, d), xown.at[3, d])
        remote(ref, ref, pown.at[0, 2], pown.at[1, 2], dev_c).start()

    def leg1(p):
        for d in range(2):
            own = tin.at[pl.ds(pl.multiple_of(d * T2 + p * TP, TP), TP)]
            dst = rz.at[d, pl.ds(pl.multiple_of(p * TP, TP), TP)]
            remote(own, dst, lsem.at[0, d, p], lsem.at[1, d, p], dev_q[d]).start()

    def leg2(p):
        for d in range(2):
            mid = rz.at[d, pl.ds(pl.multiple_of(p * TP, TP), TP)]
            wait_on(mid, lsem.at[1, d, p])
            dst = piece(c, x, 1 - zq[d] // ZL, d, p)
            remote(mid, dst, lsem.at[2, d, p], lsem.at[3, d, p], dev_q[d]).start()

    def to_partner(ref, r, h, p):
        remote(ref, ref, psem.at[0, r * 2 + h, p], psem.at[1, r * 2 + h, p], dev_c).start()

    def opp_arrived(p):
        for h in range(2):
            ref = piece(c, x, oz, h, p)
            wait_on(ref, lsem.at[3, h, p])
            for d in range(2):
                remote(ref, ref, xsem.at[d, h, p], xsem.at[2 + d, h, p], dev_x[d]).start()
            to_partner(ref, 0, h, p)

    def opp_x(p):
        for d, r in ((0, 3), (1, 1)):
            for h in (d, 1 - d):
                ref = piece(c, (x + r) % X, oz, h, p)
                wait_on(ref, xsem.at[2 + d, h, p])
                if h == d:
                    remote(ref, ref, rsem.at[0, h, p], rsem.at[1, h, p], dev_x[d]).start()
                to_partner(ref, r, h, p)

    def opp_far(p):
        for h in range(2):
            ref = piece(c, x2, oz, h, p)
            wait_on(ref, rsem.at[1, h, p])
            to_partner(ref, 2, h, p)

    for d in range(2):
        @pl.when(has_z[d])
        def _():
            G.z_send(gu_own, k, d)
    G.y_send(gu_own, k)
    own_start()

    for i in range(2):
        dn[i, pl.ds(pl.multiple_of(dp * dn_in.shape[0], dn_in.shape[0]), dn_in.shape[0]), :] = dn_in[:, i * D2 : (i + 1) * D2]
    tok[pl.ds(pl.multiple_of((zh * 2 * X + c * X + x) * T, T), T), :] = tin[...]

    NB = 2 * X * 2

    def hots():
        rows = rows_ref[...]
        lt = T.bit_length() - 1
        r = rows & (T - 1)
        core = (rows >> lt) & 1
        xx = (rows >> (lt + 1)) & (X - 1)
        hh = rows >> (lt + 3)
        rows_in = (hh * (2 * X) + core * X + xx) * T + r
        rows_out = (core * (2 * X) + xx * 2 + hh) * T + r
        rows_col = jnp.broadcast_to(rows_in, (8, CAP)).T[:, 0:1]
        gw_col[...] = jnp.broadcast_to(gw_ref[...], (8, CAP)).T[:, 0:1]

        @pl.loop(0, NB)
        def _(b):
            off = pl.multiple_of(b * T, T)
            lanes = lax.broadcasted_iota(jnp.int32, (CAP, T), 1) + b * T
            oh[:, pl.ds(off, T)] = jnp.where(rows_col == lanes, 1.0, 0.0).astype(BF)
            subs = lax.broadcasted_iota(jnp.int32, (T, CAP), 0) + b * T
            oht[pl.ds(off, T), :] = jnp.where(rows_out == subs, 1.0, 0.0).astype(BF)

    def when_in(s, lo, hi, f):
        @pl.when((s >= lo) & (s < hi))
        def _():
            f(s - lo)

    D1 = 3
    DL, A0, B0, RL = 3, 1, 2, 2

    def when_at(s, lag, f):
        v = s - (A0 + lag)

        @pl.when((v >= 0) & (v % B0 == 0) & (v // B0 < NP))
        def _():
            f(v // B0)

    def dn_step(W, s, lag):
        @pl.when(s == lag)
        def _():
            for d in range(2):
                @pl.when(has_z[d])
                def _():
                    W.z_send(W.own, k, d)
            W.y_send(W.own, k)

        when_in(s, lag + 1, lag + ZL, lambda i: W.z_step(i + 1, True))
        when_in(s, lag + RL, lag + RL + ZL, W.relay_step)

    def step(s):
        when_in(s, 1, ZL, lambda i: G.z_step(i + 1, True))
        when_at(s, 0, leg1)
        when_at(s, 1, leg2)
        when_in(s, 1, 2, lambda i: own_arrivals())
        when_at(s, 2, opp_arrived)
        when_in(s, RL, RL + ZL, G.relay_step)
        when_in(s, 2, 3, lambda i: own_far())
        when_at(s, 3, opp_x)
        when_at(s, 4, opp_far)
        dn_step(WS[0], s, DL)
        dn_step(WS[1], s, DL + D1)

    TN = min(256, D)
    NT = D // TN
    HG = 2 * X * T

    def pick(n, q, first):
        cols = pl.ds(pl.multiple_of(n * TN, TN), TN)
        ks = pl.ds(pl.multiple_of(q * HG, HG), HG)
        got = jnp.dot(oh[:, ks], tok[ks, cols], preferred_element_type=F32)
        if not first:
            got = got + picked[:, cols].astype(F32)
        picked[:, cols] = got.astype(BF)

    @pl.loop(1, 2)
    def _(s):
        step(s)

    hots()

    @pl.loop(2, 6)
    def _(s):
        step(s)

    for r in range(X):
        wait_on(blk(1 - c, (x + r) % X, zh), pown.at[1, r])

    @pl.loop(0, NT)
    def _(n):
        pick(n, zh, True)

    TAIL = A0 + 3 * B0 + 5
    END = DL + RL + ZL

    @pl.loop(6, TAIL)
    def _(s):
        step(s)

    @pl.loop(0, NP)
    def _(p):
        for r in range(X):
            for h in range(2):
                wait_on(piece(1 - c, (x + r) % X, oz, h, p), psem.at[1, r * 2 + h, p])

    @pl.loop(0, NT)
    def _(n):
        pick(n, oz, False)

    @pl.loop(TAIL, max(END, TAIL))
    def _(s):
        step(s)

    G.arrived()
    TH = min(256, H)

    @pl.loop(0, H // TH)
    def _(n):
        ga = jnp.dot(picked[...], gu[:, pl.ds(pl.multiple_of(n * TH, TH), TH)], preferred_element_type=F32)
        ub = jnp.dot(picked[...], gu[:, pl.ds(pl.multiple_of(H + n * TH, TH), TH)], preferred_element_type=F32)
        hidden[:, pl.ds(pl.multiple_of(n * TH, TH), TH)] = (ga / (1.0 + jnp.exp(-ga)) * ub).astype(BF)

    WS[0].arrived()

    HB = 2 * X * T
    TM = min(256, HB)

    def s1(n):
        cols2 = pl.ds(pl.multiple_of((n % (NC // 2)) * CW, CW), CW)
        o = jnp.dot(hidden[...], dn[n // (NC // 2), :, cols2], preferred_element_type=F32)
        contrib[...] = (gw_col[...] * o).astype(BF)

        def spread(base):
            @pl.loop(0, HB // TM)
            def _(m):
                r = pl.ds(pl.multiple_of(base + m * TM, TM), TM)
                dense[n, r, :] = jnp.dot(oht[r, :], contrib[...], preferred_element_type=F32).astype(BF)

        theirs = pl.multiple_of((1 - c) * HB, HB)
        spread(theirs)
        remote(dense.at[n, pl.ds(theirs, HB)], prcv.at[n], csem.at[n, 0], csem.at[n, 1], dev_c).start()
        spread(pl.multiple_of(c * HB, HB))

    def pblk(n, x_, q_, count=1):
        return prcv.at[n, pl.ds(pl.multiple_of((x_ * 2 + q_) * T, T), count * T)]

    def s2(n):
        wait_on(prcv.at[n], csem.at[n, 1])

        def add(i):
            b = (x2 * 2 + i) % (2 * X)
            r = pl.ds(pl.multiple_of(b * T, T), T)
            mine = dense[n, pl.ds(pl.multiple_of(c * HB + b * T, T), T), :]
            prcv[n, r, :] = (prcv[n, r, :].astype(F32) + mine.astype(F32)).astype(BF)

        pl.loop(0, 2)(add)
        for d in range(2):
            remote(pblk(n, x2, d), xrl.at[d, n], csem.at[n, 2 + d], csem.at[n, 4 + d], dev_x[d]).start()
        pl.loop(2, 2 * X)(add)

    def s3(n):
        for d, x_ in ((0, xp), (1, xm)):
            wait_on(xrl.at[d, n], csem.at[n, 4 + d])
            r = pl.ds(pl.multiple_of((x_ * 2 + d) * T, T), T)
            prcv[n, r, :] = (prcv[n, r, :].astype(F32) + xrl[d, n].astype(F32)).astype(BF)
            remote(pblk(n, x_, 0, 2), xf.at[d, n], csem.at[n, 6 + d], csem.at[n, 8 + d], dev_x[d]).start()

    def total(n, q):
        r = pl.ds(pl.multiple_of((x * 2 + q) * T, T), T)
        g = pl.ds(pl.multiple_of(q * T, T), T)
        return prcv[n, r, :].astype(F32) + xf[0, n, g, :].astype(F32) + xf[1, n, g, :].astype(F32)

    def s4(n):
        for d in range(2):
            wait_on(xf.at[d, n], csem.at[n, 8 + d])
        zsend[n] = total(n, oz).astype(BF)
        for d in range(2):
            remote(zsend.at[n, pl.ds(d * T2, T2)], zrel.at[d, n], csem.at[n, 10 + d], csem.at[n, 12 + d], dev_q[d]).start()

    def s5(n):
        for d in range(2):
            wait_on(zrel.at[d, n], csem.at[n, 12 + d])
            remote(zrel.at[d, n], zfin.at[n, pl.ds(d * T2, T2)], csem.at[n, 14 + d], csem.at[n, 16 + d], dev_q[d]).start()

    def s6(n):
        for d in range(2):
            wait_on(zfin.at[n, pl.ds(d * T2, T2)], csem.at[n, 16 + d])
        out[:, pl.ds(pl.multiple_of(n * CW, CW), CW)] = (total(n, zh) + zfin[n].astype(F32)).astype(BF)

    stages = (s1, s2, s3, s4, s5, s6)

    BEG = max(END, TAIL)

    @pl.loop(0, NC + LAGS[-1])
    def _(t):
        @pl.when(t < D1)
        def _():
            dn_step(WS[1], t + BEG, DL + D1)

        @pl.when(t == NC // 2)
        def _():
            WS[1].arrived()

        for i in reversed(range(len(stages))):
            @pl.when((t >= LAGS[i]) & (t < NC + LAGS[i]))
            def _():
                stages[i](t - LAGS[i])

    G.drain()
    WS[0].drain()
    WS[1].drain()
    for d in range(2):
        wait_sent_on(tin, xown.at[0, d])
        wait_sent_on(half(tin, d), xown.at[2, d])
    for r in range(X):
        wait_sent_on(tin, pown.at[0, r])

    @pl.loop(0, NP)
    def _(p):
        ref = tin.at[pl.ds(0, TP)]
        for h in range(2):
            wait_sent_on(ref, lsem.at[0, h, p])
            wait_sent_on(ref, lsem.at[2, h, p])
            wait_sent_on(ref, xsem.at[0, h, p])
            wait_sent_on(ref, xsem.at[1, h, p])
            wait_sent_on(ref, rsem.at[0, h, p])
            for r in range(X):
                wait_sent_on(ref, psem.at[0, r * 2 + h, p])

    @pl.loop(0, NC)
    def _(n):
        wait_sent_on(prcv.at[n], csem.at[n, 0])
        for d in range(2):
            wait_sent_on(xrl.at[d, n], csem.at[n, 2 + d])
            wait_sent_on(xf.at[d, n], csem.at[n, 6 + d])
            wait_sent_on(zrel.at[d, n], csem.at[n, 10 + d])
            wait_sent_on(zrel.at[d, n], csem.at[n, 14 + d])


def per_device(ZL, tokens, choice_rows, gate_weights, w_gate, w_up, w_down):
    T, D = tokens.shape
    H = w_gate.shape[2]
    CAP = choice_rows.shape[2]
    group = 4 * X * T
    CW = D // NC
    K = w_gate.shape[1]
    dn_in = w_down[0]
    dps = Y * ZL
    vmem = pl.BlockSpec(memory_space=pltpu.VMEM)
    return pl.pallas_call(
        functools.partial(layer_kernel, ZL),
        out_shape=jax.ShapeDtypeStruct((T, D), BF),
        in_specs=[vmem] * 6,
        out_specs=vmem,
        scratch_shapes=[
            pltpu.VMEM((CAP, 1), F32),
            pltpu.VMEM((group, D), BF),
            pltpu.VMEM((dps * K, 2 * H), BF),
            pltpu.VMEM((2, dps * dn_in.shape[0], D // 2), BF),
            pltpu.VMEM((CAP, group), BF),
            pltpu.VMEM((group, CAP), BF),
            pltpu.VMEM((CAP, D), BF),
            pltpu.VMEM((CAP, H), BF),
            pltpu.VMEM((CAP, CW), BF),
            pltpu.VMEM((NC, group, CW), BF),
            pltpu.VMEM((2, T // 2, D), BF),
            pltpu.VMEM((NC, group // 2, CW), BF),
            pltpu.VMEM((2, NC, T, CW), BF),
            pltpu.VMEM((2, NC, 2 * T, CW), BF),
            pltpu.VMEM((NC, T, CW), BF),
            pltpu.VMEM((2, NC, T // 2, CW), BF),
            pltpu.VMEM((NC, T, CW), BF),
            pltpu.SemaphoreType.DMA((11, ZL)),
            pltpu.SemaphoreType.DMA((11, ZL)),
            pltpu.SemaphoreType.DMA((11, ZL)),
            pltpu.SemaphoreType.DMA((4, 2, NP)),
            pltpu.SemaphoreType.DMA((4, 2, NP)),
            pltpu.SemaphoreType.DMA((2, 2, NP)),
            pltpu.SemaphoreType.DMA((2, 2 * X, NP)),
            pltpu.SemaphoreType.DMA((4, 2)),
            pltpu.SemaphoreType.DMA((2, X)),
            pltpu.SemaphoreType.DMA((NC, 18)),
        ],
        compiler_params=pltpu.CompilerParams(
            collective_id=0, has_side_effects=True, vmem_limit_bytes=62 * 1024 * 1024
        ),
    )(tokens, w_gate[0], w_up[0], dn_in, choice_rows[0], gate_weights[0])


def solution(mesh):
    return jax.shard_map(
        functools.partial(per_device, mesh.shape["dp"] // Y),
        mesh=mesh,
        in_specs=(
            P(("dp", "expert"), None),
            P("dp", "expert", None),
            P("dp", "expert", None),
            P("expert", "dp", None),
            P("expert", "dp", None),
            P("expert", "dp", None),
        ),
        out_specs=P(("dp", "expert"), None),
        check_vma=False,
    )
```
